32 devices in a mesh: groups: 2 (over x), tm: 16 (over z, y, core).
Axes of the slice: x: 2, y: 2, z: 4, core: 2. Of those that a mesh axis runs over, the one named last changes fastest.
Arguments:
- latent: bfloat16 [64, 8192], P('groups', 'tm'), parts along dimension 0, may hold values from -6 to 6
- w_in: bfloat16 [3, 3, 3, 16, 384], replicated, may hold values from -0.3125 to 0.3125
- b_in: float32 [384], replicated, may hold values from -3 to 3
- gain: float32 [384], replicated, may hold values from 0.1 to 1.9
- w_mid: bfloat16 [3, 3, 3, 384, 384], replicated, may hold values from -0.0625 to 0.0625
- b_mid: float32 [384], replicated, may hold values from -3 to 3
- w_time: bfloat16 [3, 384, 768], replicated, may hold values from -0.1875 to 0.1875
- b_time: float32 [768], replicated, may hold values from -3 to 3
Outputs:
- frames_up: bfloat16 [128, 16, 32, 384], P(('groups', 'tm')), parts along dimension 0
The draws below stay inside these ranges and needn't reach their ends.
There are 2 independent parts, one for each index of `groups`. The reference program is written for one: setup_inputs(seed, part) draws one part's arguments, and reference() takes and returns one part's arrays. A program takes and returns all parts, laid end to end along the dimension named above; an argument that names none is the same for every part. Nothing has to cross between parts.
All inputs are finite; a program needn't handle non-finite values.
Results may differ from the reference program's by a relative error of at most 0.012.
Values may be sent and summed in bfloat16 or wider, within the bound.
A program may use at most 128 MiB of HBM per device.

```python
import jax
import jax.numpy as jnp
from jax import lax

ZC = 16
C = 384
H = 16
W = 32
LF = 32


def shard_levels(key, dims, shards, low, high):
    factor_of, own = 1.0, jax.random.fold_in(key, 6)
    for position, shards_of in shards:
        steps = jnp.exp(jax.random.uniform(jax.random.fold_in(own, position), (shards_of,), jnp.float32, low / len(shards), high / len(shards)))
        factor_of = factor_of * jnp.repeat(steps, dims[position] // shards_of).reshape([-1 if axis == position else 1 for axis in range(len(dims))])
    return factor_of


def noise(rng, dims, scale, bound, split=(), held_as=jnp.bfloat16):
    entries = scale * jax.random.normal(rng, dims, jnp.float32)
    if split:
        entries = entries * shard_levels(rng, dims, split, -0.22, 0.18)
    return jnp.clip(entries, -bound, bound).astype(held_as)


def setup_inputs(seed: int = 0, part: int = 0) -> dict:
    streams_of = jax.random.split(jax.random.key(seed), 9)
    part_splits = jax.random.split(jax.random.fold_in(streams_of[8], part), 9)
    return {
        "latent": noise(part_splits[0], (LF, H * W * ZC), 1.0, 6.0, ((1, 16),)),
        "w_in": noise(streams_of[1], (3, 3, 3, ZC, C), (27 * ZC) ** -0.5, 0.3125),
        "b_in": noise(streams_of[2], (C,), 0.5, 3.0, (), jnp.float32),
        "gain": jnp.clip(1.0 + 0.18 * jax.random.normal(streams_of[3], (C,), jnp.float32), 0.1, 1.9),
        "w_mid": noise(streams_of[4], (3, 3, 3, C, C), (27 * C) ** -0.5, 0.0625),
        "b_mid": noise(streams_of[5], (C,), 0.5, 3.0, (), jnp.float32),
        "w_time": noise(streams_of[6], (3, C, 2 * C), (3 * C) ** -0.5, 0.1875),
        "b_time": noise(streams_of[7], (2 * C,), 0.5, 3.0, (), jnp.float32),
    }


def conv_valid(padded, weight, bias, spatial, edged):
    frames = padded.shape[0] - 2
    rows = padded.shape[1]
    inner = padded.shape[3]
    if spatial:
        margin = 0 if edged else 1
        padded = jnp.pad(padded, ((0, 0), (1, 1), (margin, margin), (0, 0)))
        taps = 3
    else:
        taps = 1
    cols = padded.shape[2] - taps + 1
    total = jnp.zeros((frames * rows * cols, weight.shape[-1]), jnp.float32)
    for step_t in range(3):
        for step_h in range(taps):
            for step_w in range(taps):
                window = padded[step_t:step_t + frames, step_h:step_h + rows, step_w:step_w + cols, :]
                if spatial:
                    kernel = weight[step_t, step_h, step_w]
                else:
                    kernel = weight[step_t]
                total = total + jnp.dot(window.reshape(-1, inner), kernel, preferred_element_type=jnp.float32)
    return (total + bias).reshape(frames, rows, cols, weight.shape[-1])

def conv_input(padded, weight, bias, edged):
    frames = padded.shape[0] - 2
    rows = padded.shape[1]
    inner = padded.shape[3]
    margin = 0 if edged else 1
    padded = jnp.pad(padded, ((0, 0), (1, 1), (margin, margin), (0, 0)))
    cols = padded.shape[2] - 2
    windows = []
    for step_t in range(3):
        for step_h in range(3):
            for step_w in range(3):
                windows.append(padded[step_t:step_t + frames, step_h:step_h + rows, step_w:step_w + cols, :])
    stacked = jnp.concatenate(windows, axis=-1).reshape(frames * rows * cols, 27 * inner)
    total = jnp.dot(stacked, weight.reshape(27 * inner, weight.shape[-1]), preferred_element_type=jnp.float32)
    return (total + bias).reshape(frames, rows, cols, weight.shape[-1])

def activate(hidden, gain):
    values = hidden.astype(jnp.float32)
    scale = jax.lax.rsqrt(lax.optimization_barrier(jnp.mean(values * values, axis=-1, keepdims=True)) + 1e-06)
    return jax.nn.silu(values * scale * gain).astype(jnp.bfloat16)

def reference(latent, w_in, b_in, gain, w_mid, b_mid, w_time, b_time):
    lat = latent.reshape(LF, H, W, ZC)
    zeros_in = jnp.zeros((2, H, W, ZC), latent.dtype)
    h0 = conv_input(jnp.concatenate([zeros_in, lat], axis=0), w_in, b_in, False).astype(jnp.bfloat16)
    act = activate(h0, gain)
    zeros_mid = jnp.zeros((2, H, W, C), jnp.bfloat16)
    h1 = (h0.astype(jnp.float32) + conv_valid(jnp.concatenate([zeros_mid, act], axis=0), w_mid, b_mid, True, False)).astype(jnp.bfloat16)
    up = conv_valid(jnp.concatenate([zeros_mid, h1], axis=0), w_time, b_time, False, False)
    paired = up.reshape(LF, H, W, 2, C).transpose(0, 3, 1, 2, 4)
    return paired.reshape(2 * LF, H, W, C).astype(jnp.bfloat16)
```

```python
import functools

import jax
import jax.numpy as jnp
from jax import lax
from jax.experimental import pallas as pl
from jax.experimental.pallas import tpu as pltpu
from jax.sharding import PartitionSpec as P

ZC = 16
C = 384
H = 16
W = 32
F = 2
KT = 64
ROW = W * ZC
WIDE = ROW + 128
MESH = pl.DeviceIdType.MESH
CHUNK = 16


def kernel(
    n, latent_ref, w_in_ref, b_in_ref, gain_ref, w_mid_ref, b_mid_ref, w_time_ref, b_time_ref,
    out_ref,
    padded, sent, got, spread, shifted, win, wmid, wtime, act3, hid, turn, own, halo,
    lat_send, lat_recv, halo_send, halo_recv, win_sem, wmid_sem, wtime_sem,
):
    me = lax.axis_index("tm")
    block = latent_ref.shape[1]
    frames = latent_ref.shape[0]
    per_row = ROW // block

    for t in range(9):
        pltpu.make_async_copy(w_in_ref.at[t], win.at[pl.ds(t * KT, 48)], win_sem.at[t]).start()
    for dt in range(3):
        for di in range(3):
            for dj in range(3):
                pltpu.make_async_copy(
                    w_mid_ref.at[dt, di, dj],
                    wmid.at[dt, pl.ds(dj * 3 * C + di * C, C)],
                    wmid_sem.at[dt * 9 + di * 3 + dj],
                ).start()
    pltpu.make_async_copy(w_time_ref, wtime, wtime_sem).start()

    barrier = pltpu.get_barrier_semaphore()

    def greet(o, carry):
        pl.semaphore_signal(
            barrier, inc=1, device_id={"tm": lax.rem(me + o, n)}, device_id_type=MESH
        )
        return carry

    lax.fori_loop(1, n, greet, 0)

    padded[pl.ds(0, 8), :] = jnp.zeros((8, block), jnp.float32)
    padded[pl.ds(frames, 16), :] = jnp.zeros((16, block), jnp.float32)
    padded[pl.ds(4, frames), :] = latent_ref[...].astype(jnp.float32)
    for d in range(n):
        sent[d] = padded[pl.ds(F * d, 8), :].astype(jnp.bfloat16)

    for t in range(9):
        win[pl.ds(t * KT + 48, 16), :] = jnp.zeros((16, C), jnp.bfloat16)
    win[pl.ds(9 * KT, KT), :] = jnp.zeros((KT, C), jnp.bfloat16)
    act3[0] = jnp.zeros(act3.shape[1:], jnp.bfloat16)
    act3[W + 1] = jnp.zeros(act3.shape[1:], jnp.bfloat16)

    pl.semaphore_wait(barrier, n - 1)

    def lat_copy(o):
        d = lax.rem(me + o, n)
        return pltpu.make_async_remote_copy(
            src_ref=sent.at[d], dst_ref=got.at[me], send_sem=lat_send.at[d],
            recv_sem=lat_recv.at[me], device_id={"tm": d}, device_id_type=MESH,
        )

    def send(o, carry):
        lat_copy(o).start()
        return carry

    lax.fori_loop(1, n, send, 0)
    got[me] = sent[me]

    def receive(o, carry):
        j = lax.rem(me + o, n)
        pltpu.make_async_remote_copy(
            src_ref=sent.at[j], dst_ref=got.at[j], send_sem=lat_send.at[j],
            recv_sem=lat_recv.at[j], device_id={"tm": j}, device_id_type=MESH,
        ).wait_recv()
        return carry

    lax.fori_loop(1, n, receive, 0)

    flat = got[...].astype(jnp.float32).reshape(n * 8, block)
    for c in range(block // 128):
        spread[c] = flat[:, c * 128 : (c + 1) * 128]
    picked = []
    for s in range(F + 4):
        parts = [
            spread[c, pl.ds(b * 8 + s, H, stride=8 * per_row), :]
            for b in range(per_row)
            for c in range(block // 128)
        ]
        parts.append(jnp.zeros((H, 128), jnp.float32))
        picked.append(jnp.concatenate(parts, axis=1))
    lat = jnp.concatenate(picked, axis=0)
    total = (F + 4) * H
    row_of = lax.broadcasted_iota(jnp.int32, (total, WIDE), 0) & (H - 1)
    for di in range(3):
        if di == 0:
            moved = jnp.where(row_of == 0, 0.0, pltpu.roll(lat, 1, 0))
        elif di == 2:
            moved = jnp.where(row_of == H - 1, 0.0, pltpu.roll(lat, total - 1, 0))
        else:
            moved = lat
        shifted[0, di] = moved
        shifted[1, di] = pltpu.roll(moved, KT, 1)

    for t in range(9):
        pltpu.make_async_copy(w_in_ref.at[t], win.at[pl.ds(t * KT, 48)], win_sem.at[t]).wait()

    wide = (F + 2) * H
    rows = 4 * wide
    first = jnp.where(me > 0, 0, 2)

    def columns(k, carry):
        lane = lax.broadcasted_iota(jnp.int32, (wide, WIDE), 1)
        even = ((lane - ZC * (k - 1)) & 127) < KT
        turnby = lax.rem(WIDE + ZC - ZC * k, WIDE)
        pieces = []
        for p in range(5):
            dt, di = divmod(2 * p, 3)
            both = shifted[0, di, pl.ds(dt * H, wide), :]
            if p < 4:
                dt, di = divmod(2 * p + 1, 3)
                both = jnp.where(even, both, shifted[1, di, pl.ds(dt * H, wide), :])
            pieces.append(pltpu.roll(both, turnby, 1)[:, :ROW].astype(jnp.bfloat16))
        left = jnp.concatenate(
            [
                jnp.concatenate([piece[:, g * 128 : (g + 1) * 128] for piece in pieces], axis=1)
                for g in range(4)
            ],
            axis=0,
        )
        h0 = jnp.dot(left, win[...], preferred_element_type=jnp.float32) + b_in_ref[...]
        h0 = h0.astype(jnp.bfloat16)
        values = h0.astype(jnp.float32)
        scale = lax.rsqrt(jnp.mean(values * values, axis=-1, keepdims=True) + 1e-06)
        v = values * scale * gain_ref[...]
        act = v / (1.0 + jnp.exp(-v))
        row = lax.broadcasted_iota(jnp.int32, (rows, C), 0)
        act = jnp.where(((row >> 4) & 3) >= first, act, 0.0)
        above = jnp.where((row & (H - 1)) == 0, 0.0, pltpu.roll(act, 1, 0))
        below = jnp.where((row & (H - 1)) == H - 1, 0.0, pltpu.roll(act, rows - 1, 0))
        trio = [x.astype(jnp.bfloat16) for x in (above, act, below)]
        for g in range(4):
            for di in range(3):
                for a in range(F + 2):
                    act3[g * 8 + k + 1, a, :, pl.ds(di * C, C)] = trio[di][
                        g * wide + a * H : g * wide + (a + 1) * H
                    ]
            for a in range(F):
                hid[g * 8 + k, a] = h0[g * wide + (a + 2) * H : g * wide + (a + 3) * H]
        return carry

    lax.fori_loop(0, 8, columns, 0)

    for dt in range(3):
        for di in range(3):
            for dj in range(3):
                pltpu.make_async_copy(
                    w_mid_ref.at[dt, di, dj],
                    wmid.at[dt, pl.ds(dj * 3 * C + di * C, C)],
                    wmid_sem.at[dt * 9 + di * 3 + dj],
                ).wait()

    after = lax.rem(me + 1, n)

    def halo_copy(m):
        f = m // (W // CHUNK)
        w0 = pl.multiple_of(lax.rem(m, W // CHUNK) * CHUNK, CHUNK)
        return pltpu.make_async_remote_copy(
            src_ref=own.at[f, :, pl.ds(w0, CHUNK)], dst_ref=halo.at[f, :, pl.ds(w0, CHUNK)],
            send_sem=halo_send.at[m], recv_sem=halo_recv.at[m],
            device_id={"tm": after}, device_id_type=MESH,
        )

    def residual(m, carry):
        f = m // (W // CHUNK)
        w0 = pl.multiple_of(lax.rem(m, W // CHUNK) * CHUNK, CHUNK)
        acc = hid[pl.ds(w0, CHUNK), f].astype(jnp.float32).reshape(CHUNK * H, C) + b_mid_ref[...]
        for dt in range(3):
            left = jnp.concatenate(
                [
                    act3[pl.ds(w0 + dj, CHUNK), f + dt].reshape(CHUNK * H, 3 * C)
                    for dj in range(3)
                ],
                axis=1,
            )
            acc = acc + jnp.dot(left, wmid[dt], preferred_element_type=jnp.float32)
        for c in range(C // 128):
            turn[c] = acc[:, c * 128 : (c + 1) * 128]
        for i in range(H):
            line = [turn[c, pl.ds(i, CHUNK, stride=H), :] for c in range(C // 128)]
            own[f, i, pl.ds(w0, CHUNK)] = jnp.concatenate(line, axis=1).astype(jnp.bfloat16)

        @pl.when(me < n - 1)
        def _():
            halo_copy(m).start()

        return carry

    chunks = F * (W // CHUNK)
    lax.fori_loop(0, chunks, residual, 0)

    pltpu.make_async_copy(w_time_ref, wtime, wtime_sem).wait()

    @pl.when(me > 0)
    def _():
        for m in range(chunks):
            halo_copy(m).wait_recv()

    @pl.when(me == 0)
    def _():
        halo[...] = jnp.zeros(halo.shape, jnp.bfloat16)

    def upsample(q, carry):
        i0 = q * 4
        blocks = [
            (halo if f < 2 else own)[f % 2, pl.ds(i0, 4)].reshape(4 * W, C) for f in range(4)
        ]
        for f in range(F):
            left = jnp.concatenate(blocks[f : f + 3], axis=1)
            up = jnp.dot(left, wtime[...], preferred_element_type=jnp.float32) + b_time_ref[...]
            up = up.astype(jnp.bfloat16)
            for s in range(2):
                out_ref[2 * f + s, pl.ds(i0, 4)] = up[:, s * C : (s + 1) * C].reshape(4, W, C)
        return carry

    lax.fori_loop(0, H // 4, upsample, 0)

    def sent_all(o, carry):
        lat_copy(o).wait_send()
        return carry

    lax.fori_loop(1, n, sent_all, 0)

    @pl.when(me < n - 1)
    def _():
        for m in range(chunks):
            halo_copy(m).wait_send()


def per_device(n, latent, w_in, b_in, gain, w_mid, b_mid, w_time, b_time):
    frames, block = latent.shape
    assert frames == F * n
    bf16, f32 = jnp.bfloat16, jnp.float32
    vmem = pl.BlockSpec(memory_space=pltpu.VMEM)
    hbm = pl.BlockSpec(memory_space=pl.ANY)
    chunks = F * (W // CHUNK)
    dma = pltpu.SemaphoreType.DMA
    return pl.pallas_call(
        functools.partial(kernel, n),
        out_shape=jax.ShapeDtypeStruct((2 * F, H, W, C), bf16),
        in_specs=[vmem, hbm, vmem, vmem, hbm, vmem, hbm, vmem],
        out_specs=vmem,
        scratch_shapes=[
            pltpu.VMEM((frames + 16, block), f32),
            pltpu.VMEM((n, 8, block), bf16),
            pltpu.VMEM((n, 8, block), bf16),
            pltpu.VMEM((block // 128, n * 8, 128), f32),
            pltpu.VMEM((2, 3, (F + 4) * H, WIDE), f32),
            pltpu.VMEM((10 * KT, C), bf16),
            pltpu.VMEM((3, 9 * C, C), bf16),
            pltpu.VMEM((3 * C, 2 * C), bf16),
            pltpu.VMEM((W + 2, F + 2, H, 3 * C), bf16),
            pltpu.VMEM((W, F, H, C), bf16),
            pltpu.VMEM((C // 128, CHUNK * H, 128), f32),
            pltpu.VMEM((F, H, W, C), bf16),
            pltpu.VMEM((F, H, W, C), bf16),
            dma((n,)), dma((n,)), dma((chunks,)), dma((chunks,)), dma((9,)), dma((27,)), dma(()),
        ],
        compiler_params=pltpu.CompilerParams(
            collective_id=0, has_side_effects=True, vmem_limit_bytes=48 * 1024 * 1024
        ),
        name="decoder_window",
    )(
        latent,
        w_in.reshape(9, 3 * ZC, C),
        b_in.reshape(1, C),
        gain.reshape(1, C),
        w_mid,
        b_mid.reshape(1, C),
        w_time.reshape(3 * C, 2 * C),
        b_time.reshape(1, 2 * C),
    )


def solution(mesh):
    n = mesh.shape["tm"]
    return jax.shard_map(
        functools.partial(per_device, n),
        mesh=mesh,
        in_specs=(P("groups", "tm"), P(), P(), P(), P(), P(), P(), P()),
        out_specs=P(("groups", "tm"), None, None, None),
        check_vma=False,
    )
```

```python
import functools

import jax
import jax.numpy as jnp
from jax import lax
from jax.experimental import pallas as pl
from jax.experimental.pallas import tpu as pltpu
from jax.sharding import PartitionSpec as P

ZC = 16
C = 384
H = 16
W = 32
F = 2
KT = 64
ROW = W * ZC
WIDE = ROW + 128
MESH = pl.DeviceIdType.MESH
CHUNK = 16


def kernel(
    n, latent_ref, w_in_ref, b_in_ref, gain_ref, w_mid_ref, b_mid_ref, w_time_ref, b_time_ref,
    out_ref,
    b_in, gain, b_mid, b_time, mine, padded, sent, got, spread, shifted, win, wmid, wtime, act_ref, hid, turn, own, halo,
    lat_send, lat_recv, halo_send, halo_recv, win_sem, wmid_sem, wtime_sem, mine_sem, vec_sem,
):
    me = lax.axis_index("tm")
    block = latent_ref.shape[1]
    frames = latent_ref.shape[0]
    per_row = ROW // block

    mine_copy = pltpu.make_async_copy(latent_ref, mine, mine_sem)
    mine_copy.start()
    vectors = ((b_in_ref, b_in), (gain_ref, gain), (b_mid_ref, b_mid), (b_time_ref, b_time))
    vec_copies = [
        pltpu.make_async_copy(src, dst, vec_sem.at[v]) for v, (src, dst) in enumerate(vectors)
    ]
    for copy in vec_copies:
        copy.start()
    for t in range(9):
        pltpu.make_async_copy(w_in_ref.at[t], win.at[pl.ds(t * KT, 48)], win_sem.at[t]).start()
    mid_copies = [
        pltpu.make_async_copy(
            w_mid_ref.at[dt, di], wmid.at[dt, :, :, pl.ds(di * C, C)], wmid_sem.at[dt * 3 + di]
        )
        for dt in range(3)
        for di in range(3)
    ]
    for copy in mid_copies:
        copy.start()
    pltpu.make_async_copy(w_time_ref, wtime, wtime_sem).start()

    barrier = pltpu.get_barrier_semaphore()

    def greet(o, carry):
        pl.semaphore_signal(
            barrier, inc=1, device_id={"tm": lax.rem(me + o, n)}, device_id_type=MESH
        )
        return carry

    lax.fori_loop(1, n, greet, 0)

    padded[pl.ds(0, 8), :] = jnp.zeros((8, block), jnp.float32)
    padded[pl.ds(frames, 16), :] = jnp.zeros((16, block), jnp.float32)
    mine_copy.wait()
    padded[pl.ds(4, frames), :] = mine[...].astype(jnp.float32)
    for d in range(n):
        sent[d] = padded[pl.ds(F * d, 8), :].astype(jnp.bfloat16)

    for t in range(9):
        win[pl.ds(t * KT + 48, 16), :] = jnp.zeros((16, C), jnp.bfloat16)
    win[pl.ds(9 * KT, KT), :] = jnp.zeros((KT, C), jnp.bfloat16)
    act_ref[0] = jnp.zeros(act_ref.shape[1:], jnp.bfloat16)
    act_ref[W + 1] = jnp.zeros(act_ref.shape[1:], jnp.bfloat16)

    pl.semaphore_wait(barrier, n - 1)

    def lat_copy(o):
        d = lax.rem(me + o, n)
        return pltpu.make_async_remote_copy(
            src_ref=sent.at[d], dst_ref=got.at[me], send_sem=lat_send.at[d],
            recv_sem=lat_recv.at[me], device_id={"tm": d}, device_id_type=MESH,
        )

    def send(o, carry):
        lat_copy(o).start()
        return carry

    lax.fori_loop(1, n, send, 0)
    got[me] = sent[me]

    def receive(o, carry):
        j = lax.rem(me + o, n)
        pltpu.make_async_remote_copy(
            src_ref=sent.at[j], dst_ref=got.at[j], send_sem=lat_send.at[j],
            recv_sem=lat_recv.at[j], device_id={"tm": j}, device_id_type=MESH,
        ).wait_recv()
        return carry

    lax.fori_loop(1, n, receive, 0)

    flat = got[...].astype(jnp.float32).reshape(n * 8, block)
    for c in range(block // 128):
        spread[c] = flat[:, c * 128 : (c + 1) * 128]
    picked = []
    for s in range(F + 4):
        parts = [
            spread[c, pl.ds(b * 8 + s, H, stride=8 * per_row), :]
            for b in range(per_row)
            for c in range(block // 128)
        ]
        parts.append(jnp.zeros((H, 128), jnp.float32))
        picked.append(jnp.concatenate(parts, axis=1))
    lat = jnp.concatenate(picked, axis=0)
    total = (F + 4) * H
    row_of = lax.broadcasted_iota(jnp.int32, (total, WIDE), 0) & (H - 1)
    for di in range(3):
        if di == 0:
            moved = jnp.where(row_of == 0, 0.0, pltpu.roll(lat, 1, 0))
        elif di == 2:
            moved = jnp.where(row_of == H - 1, 0.0, pltpu.roll(lat, total - 1, 0))
        else:
            moved = lat
        shifted[0, di] = moved
        shifted[1, di] = pltpu.roll(moved, KT, 1)

    for t in range(9):
        pltpu.make_async_copy(w_in_ref.at[t], win.at[pl.ds(t * KT, 48)], win_sem.at[t]).wait()

    for copy in vec_copies:
        copy.wait()

    wide = (F + 2) * H
    rows = 4 * wide
    first = jnp.where(me > 0, 0, 2)

    def columns(k, carry):
        lane = lax.broadcasted_iota(jnp.int32, (wide, WIDE), 1)
        even = ((lane - ZC * (k - 1)) & 127) < KT
        turnby = lax.rem(WIDE + ZC - ZC * k, WIDE)
        pieces = []
        for p in range(5):
            dt, di = divmod(2 * p, 3)
            both = shifted[0, di, pl.ds(dt * H, wide), :]
            if p < 4:
                dt, di = divmod(2 * p + 1, 3)
                both = jnp.where(even, both, shifted[1, di, pl.ds(dt * H, wide), :])
            pieces.append(pltpu.roll(both, turnby, 1)[:, :ROW].astype(jnp.bfloat16))
        left = jnp.concatenate(
            [
                jnp.concatenate([piece[:, g * 128 : (g + 1) * 128] for piece in pieces], axis=1)
                for g in range(4)
            ],
            axis=0,
        )
        h0 = jnp.dot(left, win[...], preferred_element_type=jnp.float32) + b_in[...][None, :]
        h0 = h0.astype(jnp.bfloat16)
        values = h0.astype(jnp.float32)
        scale = lax.rsqrt(jnp.mean(values * values, axis=-1, keepdims=True) + 1e-06)
        v = values * scale * gain[...][None, :]
        half = 0.5 * v
        act = half + half * jnp.tanh(half)
        row = lax.broadcasted_iota(jnp.int32, (rows, C), 0)
        act = jnp.where(((row >> 4) & 3) >= first, act, 0.0)
        act = act.astype(jnp.bfloat16)
        for g in range(4):
            act_ref[pl.ds(g * 8 + k + 1, 1)] = act[g * wide : (g + 1) * wide].reshape(
                1, F + 2, H, C
            )
            for a in range(F):
                hid[g * 8 + k, a] = h0[g * wide + (a + 2) * H : g * wide + (a + 3) * H]
        return carry

    lax.fori_loop(0, 8, columns, 0)

    for copy in mid_copies:
        copy.wait()

    after = lax.rem(me + 1, n)

    def halo_copy(m):
        f = m // (W // CHUNK)
        w0 = pl.multiple_of(lax.rem(m, W // CHUNK) * CHUNK, CHUNK)
        return pltpu.make_async_remote_copy(
            src_ref=own.at[f, :, pl.ds(w0, CHUNK)], dst_ref=halo.at[f, :, pl.ds(w0, CHUNK)],
            send_sem=halo_send.at[m], recv_sem=halo_recv.at[m],
            device_id={"tm": after}, device_id_type=MESH,
        )

    def residual(m, carry):
        f = m // (W // CHUNK)
        w0 = pl.multiple_of(lax.rem(m, W // CHUNK) * CHUNK, CHUNK)
        left = jnp.concatenate(
            [
                act_ref[pl.ds(w0 + dj, CHUNK), f + dt].reshape(CHUNK * H, C)
                for dt in range(3)
                for dj in range(3)
            ],
            axis=1,
        )
        three = jnp.dot(
            left, wmid[...].reshape(9 * C, 3 * C), preferred_element_type=jnp.float32
        )
        row = lax.broadcasted_iota(jnp.int32, (CHUNK * H, C), 0) & (H - 1)
        above = pltpu.roll(three[:, :C], 1, 0)
        below = pltpu.roll(three[:, 2 * C :], CHUNK * H - 1, 0)
        acc = hid[pl.ds(w0, CHUNK), f].astype(jnp.float32).reshape(CHUNK * H, C)
        acc = acc + b_mid[...][None, :] + three[:, C : 2 * C]
        acc = acc + jnp.where(row == 0, 0.0, above) + jnp.where(row == H - 1, 0.0, below)
        for c in range(C // 128):
            turn[c] = acc[:, c * 128 : (c + 1) * 128]
        for i in range(H):
            line = [turn[c, pl.ds(i, CHUNK, stride=H), :] for c in range(C // 128)]
            own[f, i, pl.ds(w0, CHUNK)] = jnp.concatenate(line, axis=1).astype(jnp.bfloat16)

        @pl.when(me < n - 1)
        def _():
            halo_copy(m).start()

        return carry

    chunks = F * (W // CHUNK)
    lax.fori_loop(0, chunks, residual, 0)

    pltpu.make_async_copy(w_time_ref, wtime, wtime_sem).wait()

    @pl.when(me > 0)
    def _():
        for m in range(chunks):
            halo_copy(m).wait_recv()

    @pl.when(me == 0)
    def _():
        halo[...] = jnp.zeros(halo.shape, jnp.bfloat16)

    def upsample(q, carry):
        i0 = q * 4
        blocks = [
            (halo if f < 2 else own)[f % 2, pl.ds(i0, 4)].reshape(4 * W, C) for f in range(4)
        ]
        for f in range(F):
            left = jnp.concatenate(blocks[f : f + 3], axis=1)
            up = jnp.dot(left, wtime[...], preferred_element_type=jnp.float32) + b_time[...][None, :]
            up = up.astype(jnp.bfloat16)
            for s in range(2):
                out_ref[2 * f + s, pl.ds(i0, 4)] = up[:, s * C : (s + 1) * C].reshape(4, W, C)
        return carry

    lax.fori_loop(0, H // 4, upsample, 0)

    def sent_all(o, carry):
        lat_copy(o).wait_send()
        return carry

    lax.fori_loop(1, n, sent_all, 0)

    @pl.when(me < n - 1)
    def _():
        for m in range(chunks):
            halo_copy(m).wait_send()


def per_device(n, latent, w_in, b_in, gain, w_mid, b_mid, w_time, b_time):
    frames, block = latent.shape
    assert frames == F * n
    bf16, f32 = jnp.bfloat16, jnp.float32
    vmem = pl.BlockSpec(memory_space=pltpu.VMEM)
    hbm = pl.BlockSpec(memory_space=pltpu.HBM)
    chunks = F * (W // CHUNK)
    dma = pltpu.SemaphoreType.DMA
    return pl.pallas_call(
        functools.partial(kernel, n),
        out_shape=jax.ShapeDtypeStruct((2 * F, H, W, C), bf16),
        in_specs=[hbm] * 8,
        out_specs=vmem,
        scratch_shapes=[
            pltpu.VMEM((C,), f32), pltpu.VMEM((C,), f32), pltpu.VMEM((C,), f32),
            pltpu.VMEM((2 * C,), f32),
            pltpu.VMEM((frames, block), bf16),
            pltpu.VMEM((frames + 16, block), f32),
            pltpu.VMEM((n, 8, block), bf16),
            pltpu.VMEM((n, 8, block), bf16),
            pltpu.VMEM((block // 128, n * 8, 128), f32),
            pltpu.VMEM((2, 3, (F + 4) * H, WIDE), f32),
            pltpu.VMEM((10 * KT, C), bf16),
            pltpu.VMEM((3, 3, C, 3 * C), bf16),
            pltpu.VMEM((3 * C, 2 * C), bf16),
            pltpu.VMEM((W + 2, F + 2, H, C), bf16),
            pltpu.VMEM((W, F, H, C), bf16),
            pltpu.VMEM((C // 128, CHUNK * H, 128), f32),
            pltpu.VMEM((F, H, W, C), bf16),
            pltpu.VMEM((F, H, W, C), bf16),
            dma((n,)), dma((n,)), dma((chunks,)), dma((chunks,)), dma((9,)), dma((9,)), dma(()), dma(()), dma((4,)),
        ],
        compiler_params=pltpu.CompilerParams(
            collective_id=0, has_side_effects=True, vmem_limit_bytes=64000000
        ),
        name="decoder_window",
    )(
        latent,
        w_in.reshape(9, 3 * ZC, C),
        b_in,
        gain,
        w_mid,
        b_mid,
        w_time.reshape(3 * C, 2 * C),
        b_time,
    )


def solution(mesh):
    n = mesh.shape["tm"]
    return jax.shard_map(
        functools.partial(per_device, n),
        mesh=mesh,
        in_specs=(P("groups", "tm"), P(), P(), P(), P(), P(), P(), P()),
        out_specs=P(("groups", "tm"), None, None, None),
        check_vma=False,
    )
```

```python
import functools

import jax
import jax.numpy as jnp
from jax import lax
from jax.experimental import pallas as pl
from jax.experimental.pallas import tpu as pltpu
from jax.sharding import PartitionSpec as P

ZC = 16
C = 384
H = 16
W = 32
F = 2
KT = 64
ROW = W * ZC
WIDE = ROW + 128
MESH = pl.DeviceIdType.MESH
CHUNK = 16


def kernel(
    n, latent_ref, w_in_ref, b_in_ref, gain_ref, w_mid_ref, b_mid_ref, w_time_ref, b_time_ref,
    out_ref,
    b_in, gain, b_mid, b_time, mine, padded, sent, got, spread, shifted, win, wmid, wtime, act_ref, hid, turn, part, own, halo,
    lat_send, lat_recv, halo_send, halo_recv, win_sem, wmid_sem, wtime_sem, mine_sem, vec_sem,
):
    me = lax.axis_index("tm")
    block = latent_ref.shape[1]
    frames = latent_ref.shape[0]
    per_row = ROW // block

    mine_copy = pltpu.make_async_copy(latent_ref, mine, mine_sem)
    mine_copy.start()
    vectors = ((b_in_ref, b_in), (gain_ref, gain), (b_mid_ref, b_mid), (b_time_ref, b_time))
    vec_copies = [
        pltpu.make_async_copy(src, dst, vec_sem.at[v]) for v, (src, dst) in enumerate(vectors)
    ]
    for copy in vec_copies:
        copy.start()
    for t in range(9):
        pltpu.make_async_copy(w_in_ref.at[t], win.at[pl.ds(t * KT, 48)], win_sem.at[t]).start()
    mid_copies = [
        pltpu.make_async_copy(
            w_mid_ref.at[dt, di], wmid.at[dt, :, :, pl.ds(di * C, C)], wmid_sem.at[dt * 3 + di]
        )
        for dt in range(3)
        for di in range(3)
    ]
    for copy in mid_copies:
        copy.start()
    pltpu.make_async_copy(w_time_ref, wtime, wtime_sem).start()

    barrier = pltpu.get_barrier_semaphore()

    def greet(o, carry):
        pl.semaphore_signal(
            barrier, inc=1, device_id={"tm": lax.rem(me + o, n)}, device_id_type=MESH
        )
        return carry

    lax.fori_loop(1, n, greet, 0)

    padded[pl.ds(0, 8), :] = jnp.zeros((8, block), jnp.float32)
    padded[pl.ds(frames, 16), :] = jnp.zeros((16, block), jnp.float32)
    mine_copy.wait()
    padded[pl.ds(4, frames), :] = mine[...].astype(jnp.float32)
    for d in range(n):
        sent[d] = padded[pl.ds(F * d, 8), :].astype(jnp.bfloat16)

    for t in range(9):
        win[pl.ds(t * KT + 48, 16), :] = jnp.zeros((16, C), jnp.bfloat16)
    win[pl.ds(9 * KT, KT), :] = jnp.zeros((KT, C), jnp.bfloat16)
    act_ref[0] = jnp.zeros(act_ref.shape[1:], jnp.bfloat16)
    act_ref[W + 1] = jnp.zeros(act_ref.shape[1:], jnp.bfloat16)

    pl.semaphore_wait(barrier, n - 1)

    def lat_copy(o):
        d = lax.rem(me + o, n)
        return pltpu.make_async_remote_copy(
            src_ref=sent.at[d], dst_ref=got.at[me], send_sem=lat_send.at[d],
            recv_sem=lat_recv.at[me], device_id={"tm": d}, device_id_type=MESH,
        )

    def send(o, carry):
        lat_copy(o).start()
        return carry

    lax.fori_loop(1, n, send, 0)
    got[me] = sent[me]

    def receive(o, carry):
        j = lax.rem(me + o, n)
        pltpu.make_async_remote_copy(
            src_ref=sent.at[j], dst_ref=got.at[j], send_sem=lat_send.at[j],
            recv_sem=lat_recv.at[j], device_id={"tm": j}, device_id_type=MESH,
        ).wait_recv()
        return carry

    lax.fori_loop(1, n, receive, 0)

    flat = got[...].astype(jnp.float32).reshape(n * 8, block)
    for c in range(block // 128):
        spread[c] = flat[:, c * 128 : (c + 1) * 128]
    picked = []
    for s in range(F + 4):
        parts = [
            spread[c, pl.ds(b * 8 + s, H, stride=8 * per_row), :]
            for b in range(per_row)
            for c in range(block // 128)
        ]
        parts.append(jnp.zeros((H, 128), jnp.float32))
        picked.append(jnp.concatenate(parts, axis=1))
    lat = jnp.concatenate(picked, axis=0)
    total = (F + 4) * H
    row_of = lax.broadcasted_iota(jnp.int32, (total, WIDE), 0) & (H - 1)
    for di in range(3):
        if di == 0:
            moved = jnp.where(row_of == 0, 0.0, pltpu.roll(lat, 1, 0))
        elif di == 2:
            moved = jnp.where(row_of == H - 1, 0.0, pltpu.roll(lat, total - 1, 0))
        else:
            moved = lat
        shifted[0, di] = moved
        shifted[1, di] = pltpu.roll(moved, KT, 1)

    for t in range(9):
        pltpu.make_async_copy(w_in_ref.at[t], win.at[pl.ds(t * KT, 48)], win_sem.at[t]).wait()

    for copy in vec_copies:
        copy.wait()

    wide = (F + 2) * H
    rows = 4 * wide
    first = jnp.where(me > 0, 0, 2)

    def columns(k, carry):
        lane = lax.broadcasted_iota(jnp.int32, (wide, WIDE), 1)
        even = ((lane - ZC * (k - 1)) & 127) < KT
        turnby = lax.rem(WIDE + ZC - ZC * k, WIDE)
        pieces = []
        for p in range(5):
            dt, di = divmod(2 * p, 3)
            both = shifted[0, di, pl.ds(dt * H, wide), :]
            if p < 4:
                dt, di = divmod(2 * p + 1, 3)
                both = jnp.where(even, both, shifted[1, di, pl.ds(dt * H, wide), :])
            pieces.append(pltpu.roll(both, turnby, 1)[:, :ROW].astype(jnp.bfloat16))
        left = jnp.concatenate(
            [
                jnp.concatenate([piece[:, g * 128 : (g + 1) * 128] for piece in pieces], axis=1)
                for g in range(4)
            ],
            axis=0,
        )
        h0 = jnp.dot(left, win[...], preferred_element_type=jnp.float32) + b_in[...][None, :]
        h0 = h0.astype(jnp.bfloat16)
        values = h0.astype(jnp.float32)
        scale = lax.rsqrt(jnp.mean(values * values, axis=-1, keepdims=True) + 1e-06)
        v = values * scale * gain[...][None, :]
        half = 0.5 * v
        act = half + half * jnp.tanh(half)
        row = lax.broadcasted_iota(jnp.int32, (rows, C), 0)
        act = jnp.where(((row >> 4) & 3) >= first, act, 0.0)
        act = act.astype(jnp.bfloat16)
        for g in range(4):
            act_ref[pl.ds(g * 8 + k + 1, 1)] = act[g * wide : (g + 1) * wide].reshape(
                1, F + 2, H, C
            )
            for a in range(F):
                hid[g * 8 + k, a] = h0[g * wide + (a + 2) * H : g * wide + (a + 3) * H]
        return carry

    lax.fori_loop(0, 8, columns, 0)

    for copy in mid_copies:
        copy.wait()

    after = lax.rem(me + 1, n)

    def halo_copy(m):
        f = m // (W // CHUNK)
        w0 = pl.multiple_of(lax.rem(m, W // CHUNK) * CHUNK, CHUNK)
        return pltpu.make_async_remote_copy(
            src_ref=own.at[f, :, pl.ds(w0, CHUNK)], dst_ref=halo.at[f, :, pl.ds(w0, CHUNK)],
            send_sem=halo_send.at[m], recv_sem=halo_recv.at[m],
            device_id={"tm": after}, device_id_type=MESH,
        )

    def residual(m, carry):
        f = m // (W // CHUNK)
        w0 = pl.multiple_of(lax.rem(m, W // CHUNK) * CHUNK, CHUNK)
        left = jnp.concatenate(
            [
                act_ref[pl.ds(w0 + dj, CHUNK), f + dt].reshape(CHUNK * H, C)
                for dt in range(3)
                for dj in range(3)
            ],
            axis=1,
        )
        three = jnp.dot(
            left, wmid[...].reshape(9 * C, 3 * C), preferred_element_type=jnp.float32
        )
        row = lax.broadcasted_iota(jnp.int32, (CHUNK * H, C), 0) & (H - 1)
        above = pltpu.roll(three[:, :C], 1, 0)
        below = pltpu.roll(three[:, 2 * C :], CHUNK * H - 1, 0)
        acc = hid[pl.ds(w0, CHUNK), f].astype(jnp.float32).reshape(CHUNK * H, C)
        acc = acc + b_mid[...][None, :] + three[:, C : 2 * C]
        acc = acc + jnp.where(row == 0, 0.0, above) + jnp.where(row == H - 1, 0.0, below)
        for c in range(C // 128):
            turn[c] = acc[:, c * 128 : (c + 1) * 128]
        for i in range(H):
            line = [turn[c, pl.ds(i, CHUNK, stride=H), :] for c in range(C // 128)]
            own[f, i, pl.ds(w0, CHUNK)] = jnp.concatenate(line, axis=1).astype(jnp.bfloat16)

        @pl.when(me < n - 1)
        def _():
            halo_copy(m).start()

        return carry

    chunks = F * (W // CHUNK)
    lax.fori_loop(0, chunks, residual, 0)

    pltpu.make_async_copy(w_time_ref, wtime, wtime_sem).wait()

    def upsample_own(q, carry):
        mine0, mine1 = (own[f, pl.ds(q * 4, 4)].reshape(4 * W, C) for f in range(F))
        here = pl.ds(q * 4 * W, 4 * W)
        part[0, here] = jnp.dot(
            mine0, wtime[pl.ds(2 * C, C)], preferred_element_type=jnp.float32
        )
        part[1, here] = jnp.dot(
            jnp.concatenate([mine0, mine1], axis=1),
            wtime[pl.ds(C, 2 * C)],
            preferred_element_type=jnp.float32,
        )
        return carry

    lax.fori_loop(0, H // 4, upsample_own, 0)

    @pl.when(me > 0)
    def _():
        for m in range(chunks):
            halo_copy(m).wait_recv()

    @pl.when(me == 0)
    def _():
        halo[...] = jnp.zeros(halo.shape, jnp.bfloat16)

    def upsample(q, carry):
        i0 = q * 4
        past0, past1 = (halo[f, pl.ds(i0, 4)].reshape(4 * W, C) for f in range(F))
        here = pl.ds(q * 4 * W, 4 * W)
        from_halo = (
            jnp.dot(
                jnp.concatenate([past0, past1], axis=1),
                wtime[pl.ds(0, 2 * C)],
                preferred_element_type=jnp.float32,
            ),
            jnp.dot(past1, wtime[pl.ds(0, C)], preferred_element_type=jnp.float32),
        )
        for f in range(F):
            up = from_halo[f] + part[f, here] + b_time[...][None, :]
            up = up.astype(jnp.bfloat16)
            for s in range(2):
                out_ref[2 * f + s, pl.ds(i0, 4)] = up[:, s * C : (s + 1) * C].reshape(4, W, C)
        return carry

    lax.fori_loop(0, H // 4, upsample, 0)

    def sent_all(o, carry):
        lat_copy(o).wait_send()
        return carry

    lax.fori_loop(1, n, sent_all, 0)

    @pl.when(me < n - 1)
    def _():
        for m in range(chunks):
            halo_copy(m).wait_send()


def per_device(n, latent, w_in, b_in, gain, w_mid, b_mid, w_time, b_time):
    frames, block = latent.shape
    assert frames == F * n
    bf16, f32 = jnp.bfloat16, jnp.float32
    vmem = pl.BlockSpec(memory_space=pltpu.VMEM)
    hbm = pl.BlockSpec(memory_space=pltpu.HBM)
    chunks = F * (W // CHUNK)
    dma = pltpu.SemaphoreType.DMA
    return pl.pallas_call(
        functools.partial(kernel, n),
        out_shape=jax.ShapeDtypeStruct((2 * F, H, W, C), bf16),
        in_specs=[hbm] * 8,
        out_specs=vmem,
        scratch_shapes=[
            pltpu.VMEM((C,), f32), pltpu.VMEM((C,), f32), pltpu.VMEM((C,), f32),
            pltpu.VMEM((2 * C,), f32),
            pltpu.VMEM((frames, block), bf16),
            pltpu.VMEM((frames + 16, block), f32),
            pltpu.VMEM((n, 8, block), bf16),
            pltpu.VMEM((n, 8, block), bf16),
            pltpu.VMEM((block // 128, n * 8, 128), f32),
            pltpu.VMEM((2, 3, (F + 4) * H, WIDE), f32),
            pltpu.VMEM((10 * KT, C), bf16),
            pltpu.VMEM((3, 3, C, 3 * C), bf16),
            pltpu.VMEM((3 * C, 2 * C), bf16),
            pltpu.VMEM((W + 2, F + 2, H, C), bf16),
            pltpu.VMEM((W, F, H, C), bf16),
            pltpu.VMEM((C // 128, CHUNK * H, 128), f32),
            pltpu.VMEM((F, H * W, 2 * C), f32),
            pltpu.VMEM((F, H, W, C), bf16),
            pltpu.VMEM((F, H, W, C), bf16),
            dma((n,)), dma((n,)), dma((chunks,)), dma((chunks,)), dma((9,)), dma((9,)), dma(()), dma(()), dma((4,)),
        ],
        compiler_params=pltpu.CompilerParams(
            collective_id=0, has_side_effects=True, vmem_limit_bytes=64000000
        ),
        name="decoder_window",
    )(
        latent,
        w_in.reshape(9, 3 * ZC, C),
        b_in,
        gain,
        w_mid,
        b_mid,
        w_time.reshape(3 * C, 2 * C),
        b_time,
    )


def solution(mesh):
    n = mesh.shape["tm"]
    return jax.shard_map(
        functools.partial(per_device, n),
        mesh=mesh,
        in_specs=(P("groups", "tm"), P(), P(), P(), P(), P(), P(), P()),
        out_specs=P(("groups", "tm"), None, None, None),
        check_vma=False,
    )
```
